512 devices in a mesh: grp: 16 (over z), dev: 32 (over x, y, core).
Axes of the slice: x: 4, y: 4, z: 16, core: 2. Of those that a mesh axis runs over, the one named last changes fastest.
Arguments:
- orbitals: bfloat16 [1024, 48, 2304], P(('grp', 'dev')), may hold values from -6 to 6
- offsets: int32 [1024, 3], P(('grp', 'dev')), may hold values from 0 to 23
- pick: int32 [16, 32, 16], P('grp'), may hold values from 0 to 1
- pair_local: int32 [16, 32, 2], P('grp', 'dev'), may hold values from 0 to 1
- pair_source: int32 [16, 32, 2], P('grp', 'dev'), may hold values from 0 to 15, as said below
- pair_count: int32 [16, 32, 1], P('grp', 'dev'), may hold values from 1 to 2, as said below
Outputs:
- exchange_action: float32 [1024, 110592], P('grp', 'dev')
The draws below stay inside these ranges and needn't reach their ends.
Inputs may be any that keep to these rules, and one draw needn't show every extreme that they name: pair_source[g, d, p] is never g; the two slots of one device's list name different groups. Only the first pair_count[g, d, 0] slots of a device's lists are pairs; some device lists exactly 2.
All inputs are finite; a program needn't handle non-finite values.
Results may differ from the reference program's by a relative error of at most 0.002.
Values may be sent and summed in bfloat16 or wider, within the bound.
A program may use at most 64 MiB of HBM per device.

```python
import math
import jax
import jax.numpy as jnp
from jax import lax

BOX = 48
ORB_DEV = 2
PAIRS = 2
ORBITALS = 1024
N_GRP = 16
N_DEV = 32


def draw_pair_source(key, part):
    start = jax.random.randint(jax.random.fold_in(key, 11), (N_GRP, N_DEV, 1), 0, N_GRP - 1)
    slot_index = jnp.arange(PAIRS, dtype=jnp.int32)[None, None, :]
    stride = 1 + (start + slot_index) % (N_GRP - 1)
    own_group = jnp.arange(N_GRP, dtype=jnp.int32)[:, None, None]
    return ((own_group + stride) % N_GRP).astype(jnp.int32)


def draw_pair_count(key, part):
    first_key = jax.random.fold_in(key, 23)
    second_key = jax.random.fold_in(key, 29)
    lowest = PAIRS // 2
    counted = jax.random.randint(first_key, (N_GRP, N_DEV, 1), lowest, PAIRS + 1)
    chosen = jax.random.randint(second_key, (), 0, N_GRP * N_DEV)
    flat_place = jnp.arange(N_GRP * N_DEV, dtype=jnp.int32).reshape(N_GRP, N_DEV, 1)
    return jnp.where(flat_place == chosen, PAIRS, counted).astype(jnp.int32)


def touch_ends(array, key, least, top_value):
    spot = [jax.random.randint(jax.random.fold_in(key, axis), (), 0, length) for axis, length in enumerate(array.shape)]
    main_axis = array.shape.index(max(array.shape))
    beside = spot[:main_axis] + [(spot[main_axis] + 1) % array.shape[main_axis]] + spot[main_axis + 1:]
    return array.at[tuple(spot)].set(least).at[tuple(beside)].set(top_value)


def steps_of(rng, extent, shards, low, high):
    def one(axis_at, shards_of):
        steps = jax.random.uniform(jax.random.fold_in(jax.random.fold_in(rng, 6), axis_at), (shards_of,), jnp.float32, low / len(shards), high / len(shards))
        return jnp.repeat(jnp.exp(steps), extent[axis_at] // shards_of).reshape((-1,) + (1,) * (len(extent) - axis_at - 1))

    factor_of = one(*shards[0])
    for cut in shards[1:]:
        factor_of = factor_of * one(*cut)
    return factor_of


def centred(rng, extent, deviation, most, cuts=(), kind=jnp.bfloat16):
    values = jax.random.normal(rng, extent, jnp.float32) * deviation
    if len(cuts) > 0:
        values = steps_of(rng, extent, cuts, -0.22, 0.18) * values
    return jnp.clip(values, min=-most, max=most).astype(kind)


def setup_inputs(seed: int = 0) -> dict:
    streams_of = jax.random.split(jax.random.key(seed), 7)
    return {
        "orbitals": centred(streams_of[0], (ORBITALS, BOX, BOX * BOX), 1.0, 6.0, ((0, 512),)),
        "offsets": touch_ends(jax.random.randint(streams_of[1], (ORBITALS, 3), 0, BOX // 2), jax.random.fold_in(streams_of[1], 1), 0, (BOX // 2) - 1).astype(jnp.int32),
        "pick": touch_ends(jax.random.randint(streams_of[2], (N_GRP, N_DEV, N_GRP), 0, ORB_DEV), jax.random.fold_in(streams_of[2], 1), 0, ORB_DEV - 1).astype(jnp.int32),
        "pair_local": touch_ends(jax.random.randint(streams_of[3], (N_GRP, N_DEV, PAIRS), 0, ORB_DEV), jax.random.fold_in(streams_of[3], 1), 0, ORB_DEV - 1).astype(jnp.int32),
        "pair_source": draw_pair_source(jax.random.fold_in(streams_of[6], 71), 0),
        "pair_count": draw_pair_count(jax.random.fold_in(streams_of[6], 71), 0),
    }


def tables(box_side):
    freq = jnp.arange(box_side, dtype=jnp.int32)
    angle_step = math.pi / (box_side + 1)
    phase = (freq[:, None] + 1) * (freq[None, :] + 1) % (2 * (box_side + 1))
    sine_table = math.sqrt(2.0 / (box_side + 1)) * jnp.sin(angle_step * phase.astype(jnp.float32))
    modes = 2.0 - 2.0 * jnp.cos(angle_step * (freq.astype(jnp.float32) + 1.0))
    eigen_sum = modes[:, None, None] + modes[None, :, None] + modes[None, None, :]
    return (sine_table, eigen_sum.reshape(box_side, box_side * box_side))

def turn(matrix, a_field, box_side):
    product = jnp.dot(matrix, a_field, preferred_element_type=jnp.float32, precision=lax.Precision.HIGHEST)
    return product.reshape(box_side, box_side, box_side).transpose(1, 2, 0).reshape(box_side, box_side * box_side)

def pair_terms(phi_i, phi_j, offset_gap, sine_table, eigen_sum):
    box_side = phi_i.shape[0]
    box_rows = jnp.arange(box_side, dtype=jnp.int32)
    shifters = [box_rows[:, None] + offset_gap[which_axis] == box_rows[None, :] for which_axis in range(3)]
    moved = phi_j
    for shifter in shifters:
        moved = turn(shifter.astype(jnp.bfloat16), moved, box_side).astype(jnp.bfloat16)
    moved_wide = moved.astype(jnp.float32)
    own_wide = phi_i.astype(jnp.float32)
    spectrum = own_wide * moved_wide
    for repeat in range(3):
        spectrum = turn(sine_table, spectrum, box_side)
    spectrum = spectrum / eigen_sum
    for repeat in range(3):
        spectrum = turn(sine_table, spectrum, box_side)
    own_term = spectrum * moved_wide
    backward = spectrum * own_wide
    for shifter in shifters:
        backward = turn(shifter.T.astype(jnp.float32), backward, box_side)
    return (own_term, backward)

def reference(orbitals, offsets, pick, pair_local, pair_source, pair_count):
    sine_table, eigen_sum = tables(BOX)
    box_cells = BOX * BOX * BOX
    slot_range = jnp.arange(N_GRP, dtype=jnp.int32)

    def device_step(total, flat_dev):
        grp_index = flat_dev // N_DEV
        dev_index = flat_dev % N_DEV
        own_slots = pair_local[grp_index, dev_index]
        src_slots = pair_source[grp_index, dev_index]
        listed = pair_count[grp_index, dev_index, 0]
        partner_ids = ((slot_range * N_DEV + dev_index) * ORB_DEV + pick[:, dev_index, grp_index]).astype(jnp.int32)
        first_orb = (flat_dev * ORB_DEV).astype(jnp.int32)
        own_boxes = lax.dynamic_slice_in_dim(orbitals, first_orb, ORB_DEV, 0)
        own_offs = lax.dynamic_slice_in_dim(offsets, first_orb, ORB_DEV, 0)

        def pair_step(state_pair, pair_index):

            def work(inner):
                own_sum, returned = inner
                own_slot = own_slots[pair_index]
                src_slot = src_slots[pair_index]
                partner = partner_ids[src_slot]
                offset_gap = own_offs[own_slot] - offsets[partner]
                own_term, backward = pair_terms(own_boxes[own_slot], orbitals[partner], offset_gap, sine_table, eigen_sum)
                return (own_sum.at[own_slot].add(own_term), returned.at[src_slot].add(backward))

            def keep(inner):
                return inner
            return (lax.cond(pair_index < listed, work, keep, state_pair), None)
        start = (jnp.zeros((ORB_DEV, BOX, BOX * BOX), jnp.float32), jnp.zeros((N_GRP, BOX, BOX * BOX), jnp.float32))
        (own_sum, returned), unused = lax.scan(pair_step, start, jnp.arange(PAIRS, dtype=jnp.int32))
        current = lax.dynamic_slice_in_dim(total, first_orb, ORB_DEV, 0)
        total = lax.dynamic_update_slice_in_dim(total, current + own_sum.reshape(ORB_DEV, box_cells), first_orb, 0)
        rounded = lax.optimization_barrier(returned.astype(jnp.bfloat16)).astype(jnp.float32)
        total = total.at[partner_ids].add(rounded.reshape(N_GRP, box_cells))
        return (total, None)
    total = jnp.zeros((ORBITALS, box_cells), jnp.float32)
    total, unused = lax.scan(device_step, total, jnp.arange(N_GRP * N_DEV, dtype=jnp.int32))
    return total
```

```python
import functools
import math

import jax
import jax.numpy as jnp
import numpy as np
from jax import lax
from jax.experimental import pallas as pl
from jax.experimental.pallas import tpu as pltpu
from jax.sharding import PartitionSpec as P

B = 48
H = B // 2
ROWS = H * B
PADX = 2 * B
F32, BF16, I32 = jnp.float32, jnp.bfloat16, jnp.int32
KY = 4


def host_tables():
    k = np.arange(B)
    step = math.pi / (B + 1)
    s = math.sqrt(2.0 / (B + 1)) * np.sin(step * ((k[:, None] + 1) * (k[None, :] + 1) % (2 * (B + 1))))
    modes = 2.0 - 2.0 * np.cos(step * (k + 1.0))
    s = s.astype(np.float32)
    s_hi = s.astype(jnp.bfloat16)
    s_lo = (s - s_hi.astype(np.float32)).astype(jnp.bfloat16)
    left = np.concatenate([s_hi, s_hi, s_lo], axis=1)
    right = np.zeros((2, 2, 64, 2, 2, 64), jnp.bfloat16)
    for part, m in enumerate((s_hi, s_lo)):
        for twice in range(2):
            for half in range(2):
                right[twice, half, :B, part, half, :B] = m
    right = right.reshape(256, 256)
    inv = np.zeros((H, B, 2, 64), np.float32)
    lam = modes[:, None, None] + modes[None, :, None] + modes[None, None, :]
    for half in range(2):
        inv[:, :, half, :B] = 1.0 / lam[half * H:(half + 1) * H]
    return left, right, inv.reshape(ROWS, 128)


def split(v):
    hi = v.astype(BF16)
    lo = (v - hi.astype(F32)).astype(BF16)
    return hi, lo


def sublane_stage(left, v):
    hi, lo = split(v)
    return jnp.dot(left, jnp.concatenate([hi, lo, hi], axis=0), preferred_element_type=F32)


def lane_stage(right, v):
    hi, lo = split(v)
    r = jnp.dot(jnp.concatenate([hi, lo], axis=1), right, preferred_element_type=F32)
    return r[:, :128] + r[:, 128:]


def lanes():
    return lax.broadcasted_iota(I32, (B, 128), 1)


def roll(v, shift):
    return v if isinstance(shift, int) and shift % 128 == 0 else pltpu.roll(v, shift, 1)


def rows_of(y, size=B, step=B):
    return pl.ds(pl.multiple_of(y * step, 8), size)


def unpack(box, write):
    lane = lanes()
    pad = (lane & 63) < B

    def chunk(c, carry):
        def col(v, q):
            at = pl.multiple_of((c * 3 + v + 9 * q) * 128, 128)
            return box[:, pl.ds(at, 128)].astype(F32)

        src = [[col(v, q) for v in range(3)] for q in range(2)]
        for m in range(8):
            v, o = divmod(B * m, 128)
            first = 128 - o
            parts = []
            for q in range(2):
                piece = roll(src[q][v], (64 * q - o) % 128)
                if first < B:
                    piece = jnp.where(lane < 64 * q + first, piece, roll(src[q][v + 1], (64 * q + first) % 128))
                parts.append(piece)
            write(c * 8 + m, jnp.where(pad, jnp.where(lane < 64, parts[0], parts[1]), 0.0))
        return carry

    lax.fori_loop(0, 3, chunk, 0)


def spread_into(spread, y, v):
    low = lanes() < 64
    turned = pltpu.roll(v, 64, 1)
    for at, val in ((y + H, v), (y, jnp.where(low, 0.0, turned)), (y + 2 * H, jnp.where(low, turned, 0.0))):
        spread[pl.ds(pl.multiple_of(at * PADX + H, 8), B), :] = val


def shifted(spread, y, g0, g1, g2):
    z = (lanes() & 63)
    ok = (z < B) & (z + g2 >= 0) & (z + g2 < B)
    v = spread[pl.ds((y + g1 + H) * PADX + H + g0, B), :]
    return jnp.where(ok, pltpu.roll(v, lax.rem(128 - g2, 128), 1), 0.0)


def poisson_task(typ, gaps, boxes, left, right, inv, own, moved, field, spread, acc):
    g0, g1, g2 = gaps
    lt = left[...]
    rt = right[...]

    def put_own(y, v):
        own[rows_of(y), :] = v

    unpack(boxes.at[0], put_own)
    unpack(boxes.at[1], lambda y, v: spread_into(spread, y, v))

    def forward(c, carry):
        dens = []
        for m in range(KY):
            y = c * KY + m
            mv = shifted(spread, y, g0, g1, g2)
            moved[rows_of(y), :] = mv
            dens.append(own[rows_of(y), :] * mv)
        r = sublane_stage(lt, jnp.concatenate(dens, axis=1))
        r = lane_stage(rt, jnp.concatenate([r[:, 128 * m:128 * (m + 1)] for m in range(KY)], axis=0))
        field[rows_of(c, KY * B, KY * B), :] = r
        return carry

    lax.fori_loop(0, H // KY, forward, 0)

    low = lax.broadcasted_iota(I32, (H, 128), 1) < 64

    def middle(c, carry):
        cols = []
        for m in range(KY):
            x = c * KY + m
            u = field[pl.ds(x, H, stride=B), :]
            w = field[pl.ds(x + H, H, stride=B), :]
            cols.append(jnp.concatenate(
                [jnp.where(low, u, pltpu.roll(w, 64, 1)), jnp.where(low, pltpu.roll(u, 64, 1), w)], axis=0))
        r = sublane_stage(lt, jnp.concatenate(cols, axis=1))
        r = r * jnp.concatenate([inv[rows_of(c * KY + m), :] for m in range(KY)], axis=1)
        r = sublane_stage(lt, r)
        for m in range(KY):
            x = c * KY + m
            u = r[:H, 128 * m:128 * (m + 1)]
            w = r[H:, 128 * m:128 * (m + 1)]
            field[pl.ds(x, H, stride=B), :] = jnp.where(low, u, pltpu.roll(w, 64, 1))
            field[pl.ds(x + H, H, stride=B), :] = jnp.where(low, pltpu.roll(u, 64, 1), w)
        return carry

    lax.fori_loop(0, H // KY, middle, 0)

    def backward(use):
        def step(c, carry):
            r = lane_stage(rt, field[rows_of(c, KY * B, KY * B), :])
            r = jnp.concatenate([r[B * m:B * (m + 1)] for m in range(KY)], axis=1)
            r = sublane_stage(lt, r)
            for m in range(KY):
                use(c * KY + m, r[:, 128 * m:128 * (m + 1)])
            return carry

        lax.fori_loop(0, H // KY, step, 0)

    @pl.when(typ == 0)
    def _():
        def use(y, v):
            acc[rows_of(y), :] += v * moved[rows_of(y), :]

        backward(use)

    @pl.when(typ == 1)
    def _():
        def use(y, v):
            spread_into(spread, y, (v * own[rows_of(y), :]).astype(BF16).astype(F32))

        backward(use)

        def add(y, carry):
            acc[rows_of(y), :] += shifted(spread, y, -g0, -g1, -g2)
            return carry

        lax.fori_loop(0, H, add, 0)


def pack(acc, out, base):
    lane = lanes()

    def chunk(c, carry):
        src = [acc[pl.ds(pl.multiple_of(base + (c * 8 + m) * B, 8), B), :] for m in range(8)]
        for q in range(2):
            for v in range(3):
                val = None
                for m in range(8):
                    o = B * m - 128 * v
                    if o <= -B or o >= 128:
                        continue
                    piece = roll(src[m], (o - 64 * q) % 128)
                    val = piece if val is None else jnp.where(lane >= o, piece, val)
                at = pl.multiple_of((c * 3 + v + 9 * q) * 128, 128)
                out[:, pl.ds(at, 128)] = val
        return carry

    lax.fori_loop(0, 3, chunk, 0)


G = 16


def gather_kernel(box, row, boxes, rows, send, recv, isend, irecv):
    me = lax.axis_index("grp")
    right, left = lax.rem(me + 1, G), lax.rem(me + G - 1, G)
    barrier = pltpu.get_barrier_semaphore()
    for peer in (left, right):
        pl.semaphore_signal(barrier, inc=1, device_id={"grp": peer}, device_id_type=pl.DeviceIdType.MESH)
    pl.semaphore_wait(barrier, 2)

    def hop(way, h, c):
        to = right if way == 0 else left
        src = box.at[c] if h == 1 else boxes.at[h - 1 if way == 0 else G - h + 1, c]
        dst = boxes.at[h if way == 0 else G - h, c]
        return pltpu.make_async_remote_copy(src, dst, send.at[way, h - 1, c], recv.at[way, h - 1, c],
                                            device_id={"grp": to}, device_id_type=pl.DeviceIdType.MESH)

    def ihop(way, h):
        to = right if way == 0 else left
        src = row if h == 1 else rows.at[h - 1 if way == 0 else G - h + 1]
        dst = rows.at[h if way == 0 else G - h]
        return pltpu.make_async_remote_copy(src, dst, isend.at[way, h - 1], irecv.at[way, h - 1],
                                            device_id={"grp": to}, device_id_type=pl.DeviceIdType.MESH)

    def used(way, h, c):
        return h < 8 or c == way

    def iused(way, h):
        return h < 8 or way == 0

    for h in range(1, 9):
        for way in range(2):
            if iused(way, h):
                if h > 1:
                    ihop(way, h - 1).wait_recv()
                ihop(way, h).start()
        for c in range(2):
            for way in range(2):
                cc = c if way == 0 else 1 - c
                if h > 1:
                    hop(way, h - 1, cc).wait_recv()
                if used(way, h, cc):
                    hop(way, h, cc).start()
    for way in range(2):
        hop(way, 8, way).wait_recv()
        if iused(way, 8):
            ihop(way, 8).wait_recv()
        else:
            ihop(way, 7).wait_recv()
        for h in range(1, 9):
            if iused(way, h):
                ihop(way, h).wait_send()
            for c in range(2):
                if used(way, h, c):
                    hop(way, h, c).wait_send()

def gather(box, row):
    D=pltpu.SemaphoreType.DMA
    any_ = pl.BlockSpec(memory_space=pl.ANY)
    return pl.pallas_call(gather_kernel,
        out_shape=(jax.ShapeDtypeStruct((G,)+box.shape, box.dtype), jax.ShapeDtypeStruct((G,)+row.shape,row.dtype)),
        in_specs=[any_,any_], out_specs=(any_,any_),
        scratch_shapes=[D((2,8,2)),D((2,8,2)),D((2,8)),D((2,8))],
        compiler_params=pltpu.CompilerParams(collective_id=0, has_side_effects=True, vmem_limit_bytes=16<<20))(box,row)


OFF, LOCAL, SOURCE, COUNT, PICK = 0, 6, 8, 10, 16
VMEM, SMEM, ANY = pltpu.VMEM, pltpu.SMEM, pl.ANY


def list_tasks(rows, mine, tasks, total):
    g = lax.axis_index("grp")
    total[0] = 0

    def add(kind, a, k, b, fixed, moving):
        t = total[0]
        tasks[t, 0], tasks[t, 1], tasks[t, 2], tasks[t, 3] = kind, a, k, b
        for axis in range(3):
            tasks[t, 4 + axis] = fixed(axis) - moving(axis)
        total[0] = t + 1

    def look(k, carry):
        s = lax.rem(g - k + G, G)
        for p in range(2):
            @pl.when((p < mine[0, COUNT]) & (mine[0, SOURCE + p] == s))
            def _():
                a, b = mine[0, LOCAL + p], rows[k, 0, PICK + g]
                add(0, a, k, b, lambda n: mine[0, OFF + 3 * a + n], lambda n: rows[k, 0, OFF + 3 * b + n])

            @pl.when((p < rows[k, 0, COUNT]) & (rows[k, 0, SOURCE + p] == g))
            def _():
                a, b = mine[0, PICK + s], rows[k, 0, LOCAL + p]
                add(1, a, k, b, lambda n: rows[k, 0, OFF + 3 * b + n], lambda n: mine[0, OFF + 3 * a + n])
        return carry

    lax.fori_loop(1, G, look, 0)


def pairs_kernel(rows, mine, orbitals, boxes, left, right, inv, out,
                 tasks, total, bufs, own, moved, field, spread, acc, sems):
    list_tasks(rows, mine, tasks, total)
    spread[...] = jnp.zeros_like(spread)
    acc[...] = jnp.zeros_like(acc)
    count = total[0]

    def fetch(t, slot):
        kind, a, k, b = (tasks[t, n] for n in range(4))
        return (pltpu.make_async_copy(orbitals.at[a], bufs.at[slot, kind], sems.at[slot, 0]),
                pltpu.make_async_copy(boxes.at[k, b], bufs.at[slot, 1 - kind], sems.at[slot, 1]))

    @pl.when(count > 0)
    def _():
        for c in fetch(0, 0):
            c.start()

    def one(t, carry):
        slot = lax.rem(t, 2)
        for c in fetch(t, slot):
            c.wait()

        @pl.when(t + 1 < count)
        def _():
            for c in fetch(t + 1, 1 - slot):
                c.start()

        base = pl.multiple_of(tasks[t, 1] * ROWS, 8)
        poisson_task(tasks[t, 0], [tasks[t, 4 + n] for n in range(3)], bufs.at[slot], left, right, inv,
                     own, moved, field, spread, acc.at[pl.ds(base, ROWS), :])
        return carry

    lax.fori_loop(0, count, one, 0)
    for a in range(2):
        pack(acc, out.at[a], a * ROWS)


def pairs(rows, mine, orbitals, boxes):
    left, right, inv = (jnp.asarray(t) for t in host_tables())
    spec = lambda space: pl.BlockSpec(memory_space=space)
    return pl.pallas_call(
        pairs_kernel,
        out_shape=jax.ShapeDtypeStruct((2, B, B * B), F32),
        in_specs=[spec(SMEM), spec(SMEM), spec(ANY), spec(ANY), spec(VMEM), spec(VMEM), spec(VMEM)],
        out_specs=spec(VMEM),
        scratch_shapes=[
            SMEM((40, 8), I32),
            SMEM((1,), I32),
            VMEM((2, 2, B, B * B), BF16),
            VMEM((ROWS, 128), F32),
            VMEM((ROWS, 128), F32),
            VMEM((ROWS, 128), F32),
            VMEM(((B + H) * PADX, 128), F32),
            VMEM((2 * ROWS, 128), F32),
            pltpu.SemaphoreType.DMA((2, 2)),
        ],
        compiler_params=pltpu.CompilerParams(vmem_limit_bytes=48 << 20),
    )(rows, mine, orbitals, boxes, left, right, inv)


def body(orbitals, offsets, pick, pair_local, pair_source, pair_count):
    me = lax.axis_index("dev")
    my_pick = lax.dynamic_index_in_dim(pick[0], me, 0, keepdims=False)
    pad = jnp.zeros((5,), I32)
    mine = jnp.concatenate([offsets.reshape(6), pair_local[0, 0], pair_source[0, 0], pair_count[0, 0], pad, my_pick,
                            jnp.zeros((96,), I32)]).reshape(1, 128)
    boxes, rows = gather(orbitals, mine)
    sums = pairs(rows, mine, orbitals, boxes)
    return lax.all_to_all(sums.reshape(2, B ** 3), "dev", split_axis=1, concat_axis=0, tiled=True)


def solution(mesh):
    return jax.shard_map(
        body,
        mesh=mesh,
        in_specs=(
            P(("grp", "dev"), None, None),
            P(("grp", "dev"), None),
            P("grp", None, None),
            P("grp", "dev", None),
            P("grp", "dev", None),
            P("grp", "dev", None),
        ),
        out_specs=P("grp", "dev"),
        check_vma=False,
    )
```

```python
import functools
import math

import jax
import jax.numpy as jnp
import numpy as np
from jax import lax
from jax.experimental import pallas as pl
from jax.experimental.pallas import tpu as pltpu
from jax.sharding import PartitionSpec as P

B = 48
H = B // 2
ROWS = H * B
PADX = 2 * B
F32, BF16, I32 = jnp.float32, jnp.bfloat16, jnp.int32
KY = 24


def host_tables():
    k = np.arange(B)
    step = math.pi / (B + 1)
    s = math.sqrt(2.0 / (B + 1)) * np.sin(step * ((k[:, None] + 1) * (k[None, :] + 1) % (2 * (B + 1))))
    modes = 2.0 - 2.0 * np.cos(step * (k + 1.0))
    s = s.astype(np.float32)
    s_hi = s.astype(jnp.bfloat16)
    s_lo = (s - s_hi.astype(np.float32)).astype(jnp.bfloat16)
    left = np.concatenate([s_hi, s_hi, s_lo], axis=1)
    right = np.zeros((2, 2, 64, 2, 2, 64), jnp.bfloat16)
    for part, m in enumerate((s_hi, s_lo)):
        for twice in range(2):
            for half in range(2):
                right[twice, half, :B, part, half, :B] = m
    right = right.reshape(256, 256)
    inv = np.zeros((H, B, 2, 64), np.float32)
    lam = modes[:, None, None] + modes[None, :, None] + modes[None, None, :]
    for half in range(2):
        inv[:, :, half, :B] = 1.0 / lam[half * H:(half + 1) * H]
    return left, right, inv.reshape(ROWS, 128)


def split(v):
    hi = v.astype(BF16)
    lo = (v - hi.astype(F32)).astype(BF16)
    return hi, lo


def sublane_stage(left, v):
    hi, lo = split(v)
    return jnp.dot(left, jnp.concatenate([hi, lo, hi], axis=0), preferred_element_type=F32)


def lane_stage(right, v):
    hi, lo = split(v)
    r = jnp.dot(jnp.concatenate([hi, lo], axis=1), right, preferred_element_type=F32)
    return r[:, :128] + r[:, 128:]


def lanes():
    return lax.broadcasted_iota(I32, (B, 128), 1)


def roll(v, shift):
    return v if isinstance(shift, int) and shift % 128 == 0 else pltpu.roll(v, shift, 1)


def rows_of(y, size=B, step=B):
    return pl.ds(y * step, size)


def unpack(box, write):
    lane = lanes()
    pad = (lane & 63) < B

    def chunk(c, carry):
        def col(v, q):
            at = (c * 3 + v + 9 * q) * 128
            return box[:, pl.ds(at, 128)].astype(F32)

        src = [[col(v, q) for v in range(3)] for q in range(2)]
        for m in range(8):
            v, o = divmod(B * m, 128)
            first = 128 - o
            parts = []
            for q in range(2):
                piece = roll(src[q][v], (64 * q - o) % 128)
                if first < B:
                    piece = jnp.where(lane < 64 * q + first, piece, roll(src[q][v + 1], (64 * q + first) % 128))
                parts.append(piece)
            write(c * 8 + m, jnp.where(pad, jnp.where(lane < 64, parts[0], parts[1]), 0.0))
        return carry

    for c in range(3):
        chunk(c, 0)


def spread_into(spread, y, v):
    low = lanes() < 64
    turned = pltpu.roll(v, 64, 1)
    for at, val in ((y + H, v), (y, jnp.where(low, 0.0, turned)), (y + 2 * H, jnp.where(low, turned, 0.0))):
        spread[pl.ds(at * PADX + H, B), :] = val


def shifted(spread, y, g0, g1, g2):
    z = (lanes() & 63)
    ok = (z < B) & (z + g2 >= 0) & (z + g2 < B)
    v = spread[pl.ds((y + g1 + H) * PADX + H + g0, B), :]
    return jnp.where(ok, pltpu.roll(v, lax.rem(128 - g2, 128), 1), 0.0)


def poisson_task(typ, gaps, boxes, left, right, inv, own, moved, field, spread, acc):
    g0, g1, g2 = gaps
    lt = left[...]
    rt = right[...]

    def put_own(y, v):
        own[rows_of(y), :] = v

    unpack(boxes.at[0], put_own)
    unpack(boxes.at[1], lambda y, v: spread_into(spread, y, v))

    def forward(c, carry):
        dens = []
        for m in range(KY):
            y = c * KY + m
            mv = shifted(spread, y, g0, g1, g2)
            moved[rows_of(y), :] = mv
            dens.append(own[rows_of(y), :] * mv)
        r = sublane_stage(lt, jnp.concatenate(dens, axis=1))
        r = lane_stage(rt, jnp.concatenate([r[:, 128 * m:128 * (m + 1)] for m in range(KY)], axis=0))
        field[rows_of(c, KY * B, KY * B), :] = r
        return carry

    forward(0, 0)

    low = lax.broadcasted_iota(I32, (H, 128), 1) < 64

    def middle(c, carry):
        cols = []
        for m in range(KY):
            x = c * KY + m
            u = field[pl.ds(x, H, stride=B), :]
            w = field[pl.ds(x + H, H, stride=B), :]
            cols.append(jnp.concatenate(
                [jnp.where(low, u, pltpu.roll(w, 64, 1)), jnp.where(low, pltpu.roll(u, 64, 1), w)], axis=0))
        r = sublane_stage(lt, jnp.concatenate(cols, axis=1))
        r = r * jnp.concatenate([inv[rows_of(c * KY + m), :] for m in range(KY)], axis=1)
        r = sublane_stage(lt, r)
        for m in range(KY):
            x = c * KY + m
            u = r[:H, 128 * m:128 * (m + 1)]
            w = r[H:, 128 * m:128 * (m + 1)]
            field[pl.ds(x, H, stride=B), :] = jnp.where(low, u, pltpu.roll(w, 64, 1))
            field[pl.ds(x + H, H, stride=B), :] = jnp.where(low, pltpu.roll(u, 64, 1), w)
        return carry

    middle(0, 0)

    def backward(use):
        def step(c, carry):
            r = lane_stage(rt, field[rows_of(c, KY * B, KY * B), :])
            r = jnp.concatenate([r[B * m:B * (m + 1)] for m in range(KY)], axis=1)
            r = sublane_stage(lt, r)
            for m in range(KY):
                use(c * KY + m, r[:, 128 * m:128 * (m + 1)])
            return carry

        step(0, 0)

    @pl.when(typ == 0)
    def _():
        def use(y, v):
            acc[rows_of(y), :] += v * moved[rows_of(y), :]

        backward(use)

    @pl.when(typ == 1)
    def _():
        def use(y, v):
            spread_into(spread, y, (v * own[rows_of(y), :]).astype(BF16).astype(F32))

        backward(use)

        for y in range(H):
            acc[rows_of(y), :] += shifted(spread, y, -g0, -g1, -g2)


def pack(acc, out, base):
    lane = lanes()

    def chunk(c, carry):
        src = [acc[pl.ds(base + (c * 8 + m) * B, B), :] for m in range(8)]
        for q in range(2):
            for v in range(3):
                val = None
                for m in range(8):
                    o = B * m - 128 * v
                    if o <= -B or o >= 128:
                        continue
                    piece = roll(src[m], (o - 64 * q) % 128)
                    val = piece if val is None else jnp.where(lane >= o, piece, val)
                at = (c * 3 + v + 9 * q) * 128
                out[:, pl.ds(at, 128)] = val
        return carry

    for c in range(3):
        chunk(c, 0)


G = 16


def gather_kernel(box, row, boxes, rows, send, recv, isend, irecv):
    me = lax.axis_index("grp")
    right, left = lax.rem(me + 1, G), lax.rem(me + G - 1, G)
    barrier = pltpu.get_barrier_semaphore()
    for peer in (left, right):
        pl.semaphore_signal(barrier, inc=1, device_id={"grp": peer}, device_id_type=pl.DeviceIdType.MESH)
    pl.semaphore_wait(barrier, 2)

    def hop(way, h, c):
        to = right if way == 0 else left
        src = box.at[c] if h == 1 else boxes.at[h - 1 if way == 0 else G - h + 1, c]
        dst = boxes.at[h if way == 0 else G - h, c]
        return pltpu.make_async_remote_copy(src, dst, send.at[way, h - 1, c], recv.at[way, h - 1, c],
                                            device_id={"grp": to}, device_id_type=pl.DeviceIdType.MESH)

    def ihop(way, h):
        to = right if way == 0 else left
        src = row if h == 1 else rows.at[h - 1 if way == 0 else G - h + 1]
        dst = rows.at[h if way == 0 else G - h]
        return pltpu.make_async_remote_copy(src, dst, isend.at[way, h - 1], irecv.at[way, h - 1],
                                            device_id={"grp": to}, device_id_type=pl.DeviceIdType.MESH)

    def used(way, h, c):
        return h < 8 or c == way

    def iused(way, h):
        return h < 8 or way == 0

    for h in range(1, 9):
        for way in range(2):
            if iused(way, h):
                if h > 1:
                    ihop(way, h - 1).wait_recv()
                ihop(way, h).start()
        for c in range(2):
            for way in range(2):
                cc = c if way == 0 else 1 - c
                if h > 1:
                    hop(way, h - 1, cc).wait_recv()
                if used(way, h, cc):
                    hop(way, h, cc).start()
    for way in range(2):
        hop(way, 8, way).wait_recv()
        if iused(way, 8):
            ihop(way, 8).wait_recv()
        else:
            ihop(way, 7).wait_recv()
        for h in range(1, 9):
            if iused(way, h):
                ihop(way, h).wait_send()
            for c in range(2):
                if used(way, h, c):
                    hop(way, h, c).wait_send()

def gather(box, row):
    D=pltpu.SemaphoreType.DMA
    any_ = pl.BlockSpec(memory_space=pl.ANY)
    return pl.pallas_call(gather_kernel,
        out_shape=(jax.ShapeDtypeStruct((G,)+box.shape, box.dtype), jax.ShapeDtypeStruct((G,)+row.shape,row.dtype)),
        in_specs=[any_,any_], out_specs=(any_,any_),
        scratch_shapes=[D((2,8,2)),D((2,8,2)),D((2,8)),D((2,8))],
        compiler_params=pltpu.CompilerParams(collective_id=0, has_side_effects=True, vmem_limit_bytes=67043328))(box,row)


OFF, LOCAL, SOURCE, COUNT, PICK = 0, 6, 8, 10, 16
VMEM, SMEM, ANY = pltpu.VMEM, pltpu.SMEM, pl.ANY


def list_tasks(rows, mine, tasks, total):
    g = lax.axis_index("grp")
    total[0] = 0

    def add(kind, a, k, b, fixed, moving):
        t = total[0]
        tasks[t, 0], tasks[t, 1], tasks[t, 2], tasks[t, 3] = kind, a, k, b
        for axis in range(3):
            tasks[t, 4 + axis] = fixed(axis) - moving(axis)
        total[0] = t + 1

    def look(k, carry):
        s = lax.rem(g - k + G, G)
        for p in range(2):
            @pl.when((p < mine[0, COUNT]) & (mine[0, SOURCE + p] == s))
            def _():
                a, b = mine[0, LOCAL + p], rows[k, 0, PICK + g]
                add(0, a, k, b, lambda n: mine[0, OFF + 3 * a + n], lambda n: rows[k, 0, OFF + 3 * b + n])

            @pl.when((p < rows[k, 0, COUNT]) & (rows[k, 0, SOURCE + p] == g))
            def _():
                a, b = mine[0, PICK + s], rows[k, 0, LOCAL + p]
                add(1, a, k, b, lambda n: rows[k, 0, OFF + 3 * b + n], lambda n: mine[0, OFF + 3 * a + n])
        return carry

    lax.fori_loop(1, G, look, 0)


def pairs_kernel(rows, mine, orbitals, boxes, left, right, inv, out,
                 tasks, total, bufs, own, moved, field, spread, acc, sems):
    list_tasks(rows, mine, tasks, total)
    spread[...] = jnp.zeros_like(spread)
    acc[...] = jnp.zeros_like(acc)
    count = total[0]

    def fetch(t, slot):
        kind, a, k, b = (tasks[t, n] for n in range(4))
        return (pltpu.make_async_copy(orbitals.at[a], bufs.at[slot, kind], sems.at[slot, 0]),
                pltpu.make_async_copy(boxes.at[k, b], bufs.at[slot, 1 - kind], sems.at[slot, 1]))

    @pl.when(count > 0)
    def _():
        for c in fetch(0, 0):
            c.start()

    def one(t, carry):
        slot = lax.rem(t, 2)
        for c in fetch(t, slot):
            c.wait()

        @pl.when(t + 1 < count)
        def _():
            for c in fetch(t + 1, 1 - slot):
                c.start()

        base = pl.multiple_of(tasks[t, 1] * ROWS, 8)
        poisson_task(tasks[t, 0], [tasks[t, 4 + n] for n in range(3)], bufs.at[slot], left, right, inv,
                     own, moved, field, spread, acc.at[pl.ds(base, ROWS), :])
        return carry

    lax.fori_loop(0, count, one, 0)
    for a in range(2):
        pack(acc, out.at[a], a * ROWS)


def pairs(rows, mine, orbitals, boxes):
    left, right, inv = (jnp.asarray(t) for t in host_tables())
    spec = lambda space: pl.BlockSpec(memory_space=space)
    return pl.pallas_call(
        pairs_kernel,
        out_shape=jax.ShapeDtypeStruct((2, B, B * B), F32),
        in_specs=[spec(SMEM), spec(SMEM), spec(ANY), spec(ANY), spec(VMEM), spec(VMEM), spec(VMEM)],
        out_specs=spec(VMEM),
        scratch_shapes=[
            SMEM((40, 8), I32),
            SMEM((1,), I32),
            VMEM((2, 2, B, B * B), BF16),
            VMEM((ROWS, 128), F32),
            VMEM((ROWS, 128), F32),
            VMEM((ROWS, 128), F32),
            VMEM(((B + H) * PADX, 128), F32),
            VMEM((2 * ROWS, 128), F32),
            pltpu.SemaphoreType.DMA((2, 2)),
        ],
        compiler_params=pltpu.CompilerParams(vmem_limit_bytes=67043328),
    )(rows, mine, orbitals, boxes, left, right, inv)


def body(orbitals, offsets, pick, pair_local, pair_source, pair_count):
    me = lax.axis_index("dev")
    my_pick = lax.dynamic_index_in_dim(pick[0], me, 0, keepdims=False)
    pad = jnp.zeros((5,), I32)
    mine = jnp.concatenate([offsets.reshape(6), pair_local[0, 0], pair_source[0, 0], pair_count[0, 0], pad, my_pick,
                            jnp.zeros((96,), I32)]).reshape(1, 128)
    boxes, rows = gather(orbitals, mine)
    sums = pairs(rows, mine, orbitals, boxes)
    return lax.all_to_all(sums.reshape(2, B ** 3), "dev", split_axis=1, concat_axis=0, tiled=True)


def solution(mesh):
    return jax.shard_map(
        body,
        mesh=mesh,
        in_specs=(
            P(("grp", "dev"), None, None),
            P(("grp", "dev"), None),
            P("grp", None, None),
            P("grp", "dev", None),
            P("grp", "dev", None),
            P("grp", "dev", None),
        ),
        out_specs=P("grp", "dev"),
        check_vma=False,
    )
```
